32 devices in a mesh: orb: 8 (over z, y), pair: 4 (over x, core).
Axes of the slice: x: 2, y: 2, z: 4, core: 2. Of those that a mesh axis runs over, the one named last changes fastest.
Arguments:
- orbitals: float32 [16, 32, 1024], P('orb'), may hold values from -6 to 6
- send_index: int32 [8, 4, 8], P('orb', 'pair'), may hold values from -1 to 1, as said below
- pair_left: int32 [8, 4, 8], P('orb', 'pair'), may hold values from -1 to 1, as said below
- pair_offset: int32 [8, 4, 8], P('orb', 'pair'), may hold values from -8 to 8
Outputs:
- exchange_field: float32 [16, 32, 1024], P('orb', 'pair')
The draws below stay inside these ranges and needn't reach their ends.
Inputs may be any that keep to these rules, and one draw needn't show every extreme that they name: `send_index`: -1 marks an empty route. Toward some orb index, drawn from the seed, every route from every device is live. pair_left[d, p, s + c] is -1 exactly when send_index[s, p, d + c] is -1.
All inputs are finite; a program needn't handle non-finite values.
Results may differ from the reference program's by a relative error of at most 0.0075.
Values may be sent and summed in bfloat16 or wider, within the bound.
A program may use at most 128 MiB of HBM per device.

```python
import jax
import jax.numpy as jnp
from jax import lax

B = 32
ORB_DEV = 2
CAP = 1
SWEEPS = 2
ORBITALS = 16
N_ORB = 8
N_PAIR = 4


def route_mask(key):
    base = jax.random.fold_in(key, 7)
    level_key, full_key, route_key = jax.random.split(base, 3)
    levels = 2 ** jax.random.randint(level_key, (N_PAIR, N_ORB), 0, 4)
    busiest = jax.random.randint(full_key, (), 0, N_ORB)
    levels = jnp.where(jnp.arange(N_ORB)[None, :] == busiest, 8, levels)
    draws = jax.random.randint(route_key, (N_ORB, N_PAIR, N_ORB, CAP), 0, 8)
    return draws < levels[None, :, :, None]


def draw_send_index(key, part):
    live_mask = route_mask(key)
    chosen = jax.random.randint(jax.random.fold_in(key, 11), (N_ORB, N_PAIR, N_ORB, CAP), 0, ORB_DEV)
    return jnp.where(live_mask, chosen, -1).reshape(N_ORB, N_PAIR, N_ORB * CAP).astype(jnp.int32)


def draw_pair_left(key, part):
    live_mask = jnp.transpose(route_mask(key), (2, 1, 0, 3))
    chosen = jax.random.randint(jax.random.fold_in(key, 13), (N_ORB, N_PAIR, N_ORB, CAP), 0, ORB_DEV)
    return jnp.where(live_mask, chosen, -1).reshape(N_ORB, N_PAIR, N_ORB * CAP).astype(jnp.int32)


def touch_ends(array, key, smallest, high):
    place = [jax.random.randint(jax.random.fold_in(key, axis), (), 0, length) for axis, length in enumerate(array.shape)]
    widest = array.shape.index(max(array.shape))
    next_to = place[:widest] + [(place[widest] + 1) % array.shape[widest]] + place[widest + 1:]
    return array.at[tuple(place)].set(smallest).at[tuple(next_to)].set(high)


def shard_levels(own_key, extent, pieces, smallest, top_value):
    def one(dim, shards_of):
        steps = jax.random.uniform(jax.random.fold_in(jax.random.fold_in(own_key, 6), dim), (shards_of,), jnp.float32, smallest / len(pieces), top_value / len(pieces))
        return jnp.repeat(jnp.exp(steps), extent[dim] // shards_of).reshape((-1,) + (1,) * (len(extent) - dim - 1))

    gain = one(*pieces[0])
    for cut in pieces[1:]:
        gain = gain * one(*cut)
    return gain


def gaussian(stream_key, extent, scale, limit, shards=(), kind=jnp.bfloat16):
    factor_of = shard_levels(stream_key, extent, shards, -0.22, 0.18) if shards else 1.0
    result = jax.random.normal(stream_key, extent, jnp.float32) * scale * factor_of
    return jnp.minimum(jnp.maximum(result, -limit), limit).astype(kind)


def setup_inputs(seed: int = 0) -> dict:
    key_list = jax.random.split(jax.random.key(seed), 5)
    orbitals = gaussian(key_list[0], (ORBITALS, B, B * B), 1.0, 6.0, ((0, 8),), jnp.float32)
    send_index = draw_send_index(jax.random.fold_in(key_list[4], 71), 0)
    pair_left = draw_pair_left(jax.random.fold_in(key_list[4], 71), 0)
    pair_offset = touch_ends(jax.random.randint(key_list[3], (N_ORB, N_PAIR, N_ORB * CAP), -(B // 4), B // 4 + 1), jax.random.fold_in(key_list[3], 1), -(B // 4), (B // 4 + 1) - 1).astype(jnp.int32)
    return dict(orbitals=orbitals, send_index=send_index, pair_left=pair_left, pair_offset=pair_offset)


def neighbours(field):
    box_side = field.shape[1]
    plane = field.shape[2]
    edge_x = jnp.zeros_like(field[:, :1])
    summed = jnp.concatenate([field[:, 1:], edge_x], 1) + jnp.concatenate([edge_x, field[:, :-1]], 1)
    edge_y = jnp.zeros_like(field[:, :, :box_side])
    summed = summed + jnp.concatenate([field[:, :, box_side:], edge_y], 2) + jnp.concatenate([edge_y, field[:, :, :-box_side]], 2)
    edge_z = jnp.zeros_like(field[:, :, :1])
    column = lax.broadcasted_iota(jnp.int32, (1, 1, plane), 2) % box_side
    upper = jnp.where(column < box_side - 1, jnp.concatenate([field[:, :, 1:], edge_z], 2), 0.0)
    lower = jnp.where(column > 0, jnp.concatenate([edge_z, field[:, :, :-1]], 2), 0.0)
    return summed + upper + lower


def pair_work(left, right, offsets):
    box_side = left.shape[1]
    positions = jnp.arange(box_side, dtype=jnp.int32)
    forward = (positions[None, None, :] == positions[None, :, None] - offsets[:, None, None]).astype(jnp.float32)
    shifted_right = jnp.einsum("rxw,rwc->rxc", forward, right.astype(jnp.float32), precision=lax.Precision.HIGHEST)
    left_wide = left.astype(jnp.float32)
    density = left_wide * shifted_right
    potential = jnp.zeros_like(density)
    for sweep_number in range(SWEEPS):
        potential = (neighbours(potential) + density) / 6.0
    to_left = (potential * shifted_right).astype(jnp.bfloat16)
    backward = (positions[None, None, :] == positions[None, :, None] + offsets[:, None, None]).astype(jnp.float32)
    to_right = jnp.einsum("rxw,rwc->rxc", backward, potential * left_wide, precision=lax.Precision.HIGHEST)
    return to_left, to_right.astype(jnp.bfloat16)


def reference(orbitals, send_index, pair_left, pair_offset):
    rounded = orbitals.astype(jnp.bfloat16)
    slot_count = N_ORB * CAP
    source = (jnp.arange(slot_count, dtype=jnp.int32) // CAP).astype(jnp.int32)
    total = jnp.zeros(orbitals.shape, jnp.float32)
    for pair_number in range(N_PAIR):
        def visit(accumulated, owner_index):
            zero = (owner_index * 0).astype(jnp.int32)
            pair_index = (zero + pair_number).astype(jnp.int32)
            left_rows = lax.dynamic_slice(pair_left, (owner_index, pair_index, zero), (1, 1, slot_count)).reshape(slot_count)
            offsets = lax.dynamic_slice(pair_offset, (owner_index, pair_index, zero), (1, 1, slot_count)).reshape(slot_count)
            send_rows = lax.dynamic_slice(send_index, (zero, pair_index, (owner_index * CAP).astype(jnp.int32)), (N_ORB, 1, CAP)).reshape(slot_count)
            live_mask = left_rows >= 0
            left_id = jnp.where(live_mask, owner_index * ORB_DEV + left_rows, 0).astype(jnp.int32)
            right_id = jnp.where(live_mask, source * ORB_DEV + send_rows, 0).astype(jnp.int32)
            left = jnp.where(live_mask[:, None, None], rounded[left_id], jnp.zeros((), jnp.bfloat16))
            right = jnp.where(live_mask[:, None, None], rounded[right_id], jnp.zeros((), jnp.bfloat16))
            to_left, to_right = pair_work(left, right, offsets)
            accumulated = accumulated.at[left_id].add(jnp.where(live_mask[:, None, None], to_left.astype(jnp.float32), 0.0))
            accumulated = accumulated.at[right_id].add(jnp.where(live_mask[:, None, None], to_right.astype(jnp.float32), 0.0))
            return accumulated, None

        start = jnp.zeros(orbitals.shape, jnp.float32)
        partial_value, unused = lax.scan(visit, start, jnp.arange(N_ORB, dtype=jnp.int32))
        partial_rounded = lax.optimization_barrier(partial_value.astype(jnp.bfloat16))
        total = total + partial_rounded.astype(jnp.float32)
    return -0.25 * total
```

```python
import functools

import jax
import jax.numpy as jnp
from jax import lax
from jax.experimental import pallas as pl
from jax.experimental.pallas import tpu as pltpu
from jax.sharding import PartitionSpec as P

LANES = 128
TAG = 16


def in_plane(q, box_side, lane, sub):
    group = q.shape[0]
    up = jnp.where(lane % box_side > 0, pltpu.roll(q, 1, 1), 0.0)
    down = jnp.where(lane % box_side < box_side - 1, pltpu.roll(q, LANES - 1, 1), 0.0)
    ahead = pltpu.roll(q, box_side, 1)
    ahead = jnp.where(
        lane >= box_side, ahead, jnp.where(sub > 0, pltpu.roll(ahead, 1, 0), 0.0)
    )
    behind = pltpu.roll(q, LANES - box_side, 1)
    behind = jnp.where(
        lane < LANES - box_side,
        behind,
        jnp.where(sub < group - 1, pltpu.roll(behind, group - 1, 0), 0.0),
    )
    return (up + down) + (ahead + behind)


def kernel(
    n_orb,
    n_pair,
    orb_ref,
    send_ref,
    left_ref,
    off_ref,
    out_ref,
    staged,
    boxes,
    padded_right,
    product,
    left_sum,
    out_a,
    in_a,
    out_b,
    in_b,
    out_l,
    in_l,
    out_d,
    in_d,
    own_d,
    send_a,
    recv_a,
    send_b,
    recv_b,
    send_l,
    recv_l,
    send_d,
    recv_d,
):
    owned, box_side, plane = orb_ref.shape
    group = plane // LANES
    pad = box_side // 4
    own_rows = box_side // n_pair
    part_rows = own_rows * group
    me = lax.axis_index("orb")
    my_pair = lax.axis_index("pair")

    barrier = pltpu.get_barrier_semaphore()

    def greet_orb(k, c):
        pl.semaphore_signal(barrier, inc=1, device_id={"orb": lax.rem(me + k, n_orb)})
        return c

    def greet_pair(k, c):
        pl.semaphore_signal(barrier, inc=1, device_id={"pair": lax.rem(my_pair + k, n_pair)})
        return c

    lax.fori_loop(1, n_orb, greet_orb, 0)
    lax.fori_loop(1, n_pair, greet_pair, 0)

    for b in range(owned):
        for c in range(group):
            piece = orb_ref[b, :, c * LANES : (c + 1) * LANES]
            staged[pl.ds(b * box_side * group + c, box_side, stride=group), :] = piece
    boxes[:box_side] = jnp.zeros((box_side, group, LANES), jnp.float32)
    for i in range(owned * box_side // 8):
        piece = staged[pl.ds(i * 8 * group, 8 * group), :]
        piece = piece.astype(jnp.bfloat16).astype(jnp.float32)
        boxes[pl.ds(box_side + i * 8, 8)] = piece.reshape(8, group, LANES)
    zeros = jnp.zeros((pad, group, LANES), jnp.float32)
    for ref in (padded_right, product):
        ref[:pad] = zeros
        ref[pad + box_side :] = zeros
    left_sum[...] = jnp.zeros(left_sum.shape, jnp.float32)

    def select(peer, dst):
        pick = send_ref[0, 0, peer]
        base = (pick + 1) * box_side
        for i in range(box_side // 8):
            v = boxes[pl.ds(base + i * 8, 8)].reshape(8 * group, LANES)
            dst[pl.ds(i * 8 * group, 8 * group), :] = v.astype(jnp.bfloat16)
        dst[pl.ds(box_side * group, TAG), :] = jnp.full(
            (TAG, LANES), pick, jnp.int32
        ).astype(jnp.float32).astype(jnp.bfloat16)

    def build(k, c):
        peer = lax.rem(me + k, n_orb)
        select(peer, out_a.at[peer])
        return c

    lax.fori_loop(1, n_orb, build, 0)
    select(me, in_a.at[me])
    pl.semaphore_wait(barrier, n_orb - 1 + n_pair - 1)

    def copy_a(src, dst, peer):
        return pltpu.make_async_remote_copy(
            src_ref=out_a.at[src],
            dst_ref=in_a.at[dst],
            send_sem=send_a.at[src],
            recv_sem=recv_a.at[dst],
            device_id={"orb": peer},
        )

    def start_a(k, c):
        peer = lax.rem(me + k, n_orb)
        copy_a(peer, me, peer).start()
        return c

    lax.fori_loop(1, n_orb, start_a, 0)

    lane = lax.broadcasted_iota(jnp.int32, (group, LANES), 1)
    sub = lax.broadcasted_iota(jnp.int32, (group, LANES), 0)
    sixth = 1.0 / 6.0

    def copy_b(s, q, dst):
        return pltpu.make_async_remote_copy(
            src_ref=out_b.at[s, q],
            dst_ref=in_b.at[s, dst],
            send_sem=send_b.at[s, q],
            recv_sem=recv_b.at[s, dst],
            device_id={"pair": q},
        )

    def compute(s):
        t = off_ref[0, 0, s]
        pick = left_ref[0, 0, s]
        base = (pick + 1) * box_side
        picked = jnp.full((group, LANES), pick, jnp.int32)
        masks = [picked == b for b in range(owned)]
        for i in range(box_side // 8):
            v = in_a[s, pl.ds(i * 8 * group, 8 * group), :].astype(jnp.float32)
            padded_right[pl.ds(pad + i * 8, 8)] = v.reshape(8, group, LANES)

        def load(x):
            right = padded_right[pad + x - t]
            left = boxes[base + x]
            return left, right, left * right

        nothing = jnp.zeros((group, LANES), jnp.float32)
        previous, (left, right, q) = nothing, load(0)
        for x in range(box_side):
            later = load(x + 1) if x + 1 < box_side else (None, None, nothing)
            around = in_plane(q, box_side, lane, sub) + (previous + later[2])
            potential = (around * sixth + q) * sixth
            to_left = potential * right
            for b in range(owned):
                row = b * box_side + x
                left_sum[row] = left_sum[row] + jnp.where(masks[b], to_left, 0.0)
            product[pad + x] = potential * left
            previous, (left, right, q) = q, later
        for q in range(n_pair):
            v = product[pl.ds(pad + q * own_rows + t, own_rows)]
            out_b[s, q, pl.ds(0, part_rows), :] = v.reshape(part_rows, LANES).astype(jnp.bfloat16)
            out_b[s, q, pl.ds(part_rows, TAG), :] = in_a[s, pl.ds(box_side * group, TAG), :]

        def send(j, c):
            copy_b(s, lax.rem(my_pair + j, n_pair), my_pair).start()
            return c

        lax.fori_loop(1, n_pair, send, 0)

    def gathered(s):
        def wait(j, c):
            copy_b(s, lax.rem(my_pair + j, n_pair), lax.rem(my_pair + j, n_pair)).wait_recv()
            return c

        lax.fori_loop(1, n_pair, wait, 0)

        total = [jnp.zeros((part_rows, LANES), jnp.float32) for _ in range(owned)]
        for j in range(n_pair):
            if j == 0:
                block = out_b[s, my_pair, :, :]
            else:
                block = in_b[s, lax.rem(my_pair + j, n_pair), :, :]
            value = block[:part_rows].astype(jnp.float32)
            tag = block[part_rows : part_rows + 8 * 2].astype(jnp.float32)[:8]
            for b in range(owned):
                mask = jnp.concatenate([tag == b] * (part_rows // 8), 0)
                total[b] = total[b] + jnp.where(mask, value, 0.0)
        return total

    def copy_d(src, dst, peer):
        return pltpu.make_async_remote_copy(
            src_ref=out_d.at[src],
            dst_ref=in_d.at[dst],
            send_sem=send_d.at[src],
            recv_sem=recv_d.at[dst],
            device_id={"orb": peer},
        )

    def finish(s):
        total = gathered(s)
        for b in range(owned):
            out_d[s, pl.ds(b * part_rows, part_rows), :] = total[b].astype(jnp.bfloat16)
        copy_d(s, me, s).start()

    compute(me)

    def step(k, c):
        s = lax.rem(me + n_orb - k, n_orb)
        copy_a(s, s, s).wait_recv()
        compute(s)

        @pl.when(k > 1)
        def _():
            finish(lax.rem(me + n_orb - k + 1, n_orb))

        return c

    lax.fori_loop(1, n_orb, step, 0)

    def copy_l(q, dst):
        return pltpu.make_async_remote_copy(
            src_ref=out_l.at[q],
            dst_ref=in_l.at[dst],
            send_sem=send_l.at[q],
            recv_sem=recv_l.at[dst],
            device_id={"pair": q},
        )

    for q in range(n_pair):
        for b in range(owned):
            v = left_sum[pl.ds(b * box_side + q * own_rows, own_rows)]
            out_l[q, pl.ds(b * part_rows, part_rows), :] = v.reshape(part_rows, LANES).astype(
                jnp.bfloat16
            )

    def send_left(j, c):
        copy_l(lax.rem(my_pair + j, n_pair), my_pair).start()
        return c

    lax.fori_loop(1, n_pair, send_left, 0)
    finish(lax.rem(me + 1, n_orb))

    total = gathered(me)

    def wait_left(j, c):
        q = lax.rem(my_pair + j, n_pair)
        copy_l(q, q).wait_recv()
        return c

    lax.fori_loop(1, n_pair, wait_left, 0)
    for b in range(owned):
        rows = pl.ds(b * part_rows, part_rows)
        value = total[b] + out_l[my_pair, rows, :].astype(jnp.float32)
        for j in range(1, n_pair):
            value = value + in_l[lax.rem(my_pair + j, n_pair), rows, :].astype(jnp.float32)
        own_d[rows, :] = value

    def add(k, c):
        s = lax.rem(me + n_orb - k, n_orb)
        copy_d(s, s, s).wait_recv()
        own_d[...] = own_d[...] + in_d[s, :, :].astype(jnp.float32)
        return c

    lax.fori_loop(1, n_orb, add, 0)
    for b in range(owned):
        for c in range(group):
            out_ref[b, :, c * LANES : (c + 1) * LANES] = own_d[
                pl.ds(b * part_rows + c, own_rows, stride=group), :
            ]

    def drain(k, c):
        peer = lax.rem(me + k, n_orb)
        copy_a(peer, me, peer).wait_send()
        copy_d(peer, me, peer).wait_send()
        return c

    lax.fori_loop(1, n_orb, drain, 0)

    def drain_pairs(s, c):
        def one(j, c):
            copy_b(s, lax.rem(my_pair + j, n_pair), my_pair).wait_send()
            return c

        return lax.fori_loop(1, n_pair, one, c)

    lax.fori_loop(0, n_orb, drain_pairs, 0)

    def drain_left(j, c):
        copy_l(lax.rem(my_pair + j, n_pair), my_pair).wait_send()
        return c

    lax.fori_loop(1, n_pair, drain_left, 0)


def local(n_orb, n_pair, orbitals, send_index, pair_left, pair_offset):
    owned, box_side, plane = orbitals.shape
    group = plane // LANES
    pad = box_side // 4
    rows = box_side * group
    part_rows = rows // n_pair
    smem = pl.BlockSpec(memory_space=pltpu.SMEM)
    vmem = pl.BlockSpec(memory_space=pltpu.VMEM)
    bf16, f32 = jnp.bfloat16, jnp.float32
    dma = pltpu.SemaphoreType.DMA
    field = pl.pallas_call(
        functools.partial(kernel, n_orb, n_pair),
        out_shape=jax.ShapeDtypeStruct((owned, box_side // n_pair, plane), f32),
        in_specs=[vmem, smem, smem, smem],
        out_specs=vmem,
        scratch_shapes=[
            pltpu.VMEM((owned * rows, LANES), f32),
            pltpu.VMEM(((owned + 1) * box_side, group, LANES), f32),
            pltpu.VMEM((box_side + 2 * pad, group, LANES), f32),
            pltpu.VMEM((box_side + 2 * pad, group, LANES), f32),
            pltpu.VMEM((owned * box_side, group, LANES), f32),
            pltpu.VMEM((n_orb, rows + TAG, LANES), bf16),
            pltpu.VMEM((n_orb, rows + TAG, LANES), bf16),
            pltpu.VMEM((n_orb, n_pair, part_rows + TAG, LANES), bf16),
            pltpu.VMEM((n_orb, n_pair, part_rows + TAG, LANES), bf16),
            pltpu.VMEM((n_pair, owned * part_rows, LANES), bf16),
            pltpu.VMEM((n_pair, owned * part_rows, LANES), bf16),
            pltpu.VMEM((n_orb, owned * part_rows, LANES), bf16),
            pltpu.VMEM((n_orb, owned * part_rows, LANES), bf16),
            pltpu.VMEM((owned * part_rows, LANES), f32),
            dma((n_orb,)),
            dma((n_orb,)),
            dma((n_orb, n_pair)),
            dma((n_orb, n_pair)),
            dma((n_pair,)),
            dma((n_pair,)),
            dma((n_orb,)),
            dma((n_orb,)),
        ],
        compiler_params=pltpu.CompilerParams(
            collective_id=0, has_side_effects=True, vmem_limit_bytes=67043328 if n_orb > 32 else None
        ),
        name="exchange",
    )(orbitals, send_index, pair_left, pair_offset)
    return -0.25 * field


def solution(mesh):
    n_orb, n_pair = mesh.shape["orb"], mesh.shape["pair"]
    return jax.shard_map(
        functools.partial(local, n_orb, n_pair),
        mesh=mesh,
        in_specs=(
            P("orb", None, None),
            P("orb", "pair", None),
            P("orb", "pair", None),
            P("orb", "pair", None),
        ),
        out_specs=P("orb", "pair", None),
        check_vma=False,
    )
```

```python
import functools

import jax
import jax.numpy as jnp
from jax import lax
from jax.experimental import pallas as pl
from jax.experimental.pallas import tpu as pltpu
from jax.sharding import PartitionSpec as P

LANES = 128
SUBS = 8
SEND, LEFT, OFFSET = 0, 1, 2


def kernel(
    n_orb,
    n_pair,
    orb_ref,
    send_ref,
    left_ref,
    off_ref,
    out_ref,
    left_boxes,
    right_boxes,
    dens,
    prod,
    left_sum,
    right_sum,
    in_a,
    out_d,
    in_d,
    out_t,
    in_t,
    tab_pair,
    tab_orb,
    idx_pair,
    idx_orb,
    send_a,
    recv_a,
    send_d,
    recv_d,
    send_t,
    recv_t,
    send_p,
    recv_p,
    send_i,
    recv_i,
    local_sem,
):
    owned, box_side, plane = orb_ref.shape
    groups = plane // n_pair // LANES
    pad = box_side // 4
    own_rows = box_side // n_pair
    f32, bf16 = jnp.float32, jnp.bfloat16
    me = lax.axis_index("orb")
    mine = lax.axis_index("pair")
    barrier = pltpu.get_barrier_semaphore()

    def each_orb(body):
        lax.fori_loop(1, n_orb, lambda k, c: (body(lax.rem(me + k, n_orb)), c)[1], 0)

    def each_back(body):
        lax.fori_loop(1, n_orb, lambda k, c: (body(lax.rem(me + n_orb - k, n_orb)), c)[1], 0)

    def each_pair(body):
        lax.fori_loop(1, n_pair, lambda k, c: (body(lax.rem(mine + k, n_pair)), c)[1], 0)

    each_orb(lambda o: pl.semaphore_signal(barrier, inc=1, device_id={"orb": o}))
    each_pair(lambda q: pl.semaphore_signal(barrier, inc=1, device_id={"pair": q}))

    tab_pair[SEND, mine] = send_ref[0]
    tab_pair[LEFT, mine] = left_ref[0]
    tab_pair[OFFSET, mine] = off_ref[0]

    lane = lax.broadcasted_iota(jnp.int32, (box_side, LANES), 1)
    first = mine * groups
    below = jnp.maximum(first - 1, 0)
    above = jnp.minimum(first + groups, groups * n_pair - 1)

    def column(b, c):
        at = pl.ds(pl.multiple_of(c * LANES, LANES), LANES)
        return orb_ref[b, :, at].astype(bf16).astype(f32)

    left_boxes[0] = jnp.zeros(left_boxes.shape[1:], f32)
    right_boxes[...] = jnp.zeros(right_boxes.shape, f32)
    halos = []
    for b in range(owned):
        for g in range(groups):
            piece = column(b, first + g)
            left_boxes[b + 1, g] = piece
            in_a[me, b * groups + g] = piece.astype(bf16)
        has_below = lane + jnp.where(mine > 0, 0, LANES) < box_side
        has_above = lane - jnp.where(mine < n_pair - 1, 0, LANES) >= LANES - box_side
        halo = jnp.where(has_below, pltpu.roll(column(b, below), box_side, 1), 0.0)
        halo = jnp.where(
            has_above, pltpu.roll(column(b, above), LANES - box_side, 1), halo
        )
        left_boxes[b + 1, groups] = halo
        halos.append(halo if b == 0 else pltpu.roll(halo, b * 2 * box_side, 1))
    in_a[me, owned * groups] = functools.reduce(jnp.add, halos).astype(bf16)
    dens[...] = jnp.zeros(dens.shape, f32)
    prod[...] = jnp.zeros(prod.shape, f32)
    left_sum[...] = jnp.zeros(left_sum.shape, f32)

    pl.semaphore_wait(barrier, n_orb - 1 + n_pair - 1)

    def copy_p(q, row):
        return pltpu.make_async_remote_copy(
            src_ref=tab_pair.at[:, mine],
            dst_ref=tab_pair.at[:, row],
            send_sem=send_p.at[q],
            recv_sem=recv_p.at[row],
            device_id={"pair": q},
        )

    def copy_a(o, slot):
        return pltpu.make_async_remote_copy(
            src_ref=in_a.at[me],
            dst_ref=in_a.at[slot],
            send_sem=send_a.at[o],
            recv_sem=recv_a.at[slot],
            device_id={"orb": o},
        )

    def copy_i(o, slot):
        return pltpu.make_async_remote_copy(
            src_ref=tab_pair.at[SEND],
            dst_ref=tab_orb.at[slot],
            send_sem=send_i.at[o],
            recv_sem=recv_i.at[slot],
            device_id={"orb": o},
        )

    def copy_d(o, slot):
        return pltpu.make_async_remote_copy(
            src_ref=out_d.at[o],
            dst_ref=in_d.at[slot],
            send_sem=send_d.at[o],
            recv_sem=recv_d.at[slot],
            device_id={"orb": o},
        )

    def copy_t(q, slot):
        return pltpu.make_async_remote_copy(
            src_ref=out_t.at[q],
            dst_ref=in_t.at[slot],
            send_sem=send_t.at[q],
            recv_sem=recv_t.at[slot],
            device_id={"pair": q},
        )

    each_pair(lambda q: copy_p(q, mine).start())
    each_orb(lambda o: copy_a(o, me).start())
    each_pair(lambda q: copy_p(q, q).wait_recv())
    each_orb(lambda o: copy_i(o, me).start())
    tab_orb[me] = tab_pair[SEND]
    fetch = pltpu.make_async_copy(tab_pair, idx_pair, local_sem)
    fetch.start()
    fetch.wait()

    tile = (SUBS, LANES)
    lane = lax.broadcasted_iota(jnp.int32, tile, 1)
    inner_up = lane % box_side > 0
    inner_down = lane % box_side < box_side - 1
    from_here_up = lane >= box_side
    from_here_down = lane < LANES - box_side
    sixth = 1.0 / 6.0
    steps = box_side // SUBS

    def process(s, right_index):
        for b in range(owned):
            for g in range(groups):
                right_boxes[b + 1, g, pl.ds(pad, box_side), :] = in_a[s, b * groups + g].astype(f32)
            halo = in_a[s, owned * groups].astype(f32)
            if b:
                halo = pltpu.roll(halo, LANES - b * 2 * box_side, 1)
            right_boxes[b + 1, groups, pl.ds(pad, box_side), :] = halo
        right_sum[...] = jnp.zeros(right_sum.shape, f32)

        def route(p, c):
            right_pick = right_index(p)
            left_pick = idx_pair[LEFT, p, 0, s]
            t = idx_pair[OFFSET, p, 0, s]
            left_tile = jnp.full(tile, left_pick, jnp.int32)
            right_tile = jnp.full(tile, right_pick, jnp.int32)
            rights, lefts, q = {}, {}, {}
            for i in range(steps):
                for g in range(groups + 1):
                    right = right_boxes[right_pick + 1, g, pl.ds(pad + i * SUBS - t, SUBS), :]
                    left = left_boxes[left_pick + 1, g, pl.ds(i * SUBS, SUBS), :]
                    q[i, g] = left * right
                    if g < groups:
                        dens[g, pl.ds((i + 1) * SUBS, SUBS), :] = q[i, g]
                        rights[i, g], lefts[i, g] = right, left
            for i in range(steps):
                ups = [pltpu.roll(q[i, g], box_side, 1) for g in range(groups)]
                downs = [pltpu.roll(q[i, g], LANES - box_side, 1) for g in range(groups)]
                for g in range(groups):
                    here = q[i, g]
                    up = jnp.where(from_here_up, ups[g], ups[g - 1] if g else q[i, groups])
                    down = jnp.where(
                        from_here_down,
                        downs[g],
                        downs[g + 1] if g + 1 < groups else q[i, groups],
                    )
                    fore = jnp.where(inner_up, pltpu.roll(here, 1, 1), 0.0)
                    back = jnp.where(inner_down, pltpu.roll(here, LANES - 1, 1), 0.0)
                    before = dens[g, pl.ds((i + 1) * SUBS - 1, SUBS), :]
                    after = dens[g, pl.ds((i + 1) * SUBS + 1, SUBS), :]
                    around = (up + down) + (fore + back) + (before + after)
                    potential = (around * sixth + here) * sixth
                    to_left = potential * rights[i, g]
                    at = pl.ds(i * SUBS, SUBS)
                    for b in range(owned):
                        left_sum[b, g, at, :] = left_sum[b, g, at, :] + jnp.where(
                            left_tile == b, to_left, 0.0
                        )
                    prod[g, pl.ds(pad + i * SUBS, SUBS), :] = potential * lefts[i, g]
            for i in range(steps):
                at = pl.ds(i * SUBS, SUBS)
                for g in range(groups):
                    value = prod[g, pl.ds(pad + i * SUBS + t, SUBS), :]
                    for b in range(owned):
                        right_sum[b, g, at, :] = right_sum[b, g, at, :] + jnp.where(
                            right_tile == b, value, 0.0
                        )
            return c

        lax.fori_loop(0, n_pair, route, 0)

    process(me, lambda p: idx_pair[SEND, p, 0, me])
    left_sum[...] = left_sum[...] + right_sum[...]

    each_orb(lambda o: copy_i(o, o).wait_recv())
    fetch_orb = pltpu.make_async_copy(tab_orb, idx_orb, local_sem)
    fetch_orb.start()
    fetch_orb.wait()

    def slot(s):
        copy_a(s, s).wait_recv()
        process(s, lambda p: idx_orb[s, p, 0, me])
        out_d[s] = right_sum[...].astype(bf16)
        copy_d(s, me).start()

    each_back(slot)

    def add(s):
        copy_d(s, s).wait_recv()
        left_sum[...] = left_sum[...] + in_d[s].astype(f32)

    each_orb(add)

    blocks = owned * groups
    for q in range(n_pair):
        rows = left_sum[:, :, q * own_rows : (q + 1) * own_rows, :]
        out_t[q] = rows.reshape(blocks * own_rows, LANES).astype(bf16)
    in_t[mine] = out_t[mine]
    each_pair(lambda q: copy_t(q, mine).start())
    each_pair(lambda q: copy_t(q, q).wait_recv())
    for q in range(n_pair):
        rows = in_t[q].astype(f32)
        for b in range(owned):
            for g in range(groups):
                at = (b * groups + g) * own_rows
                out_ref[b, :, (q * groups + g) * LANES : (q * groups + g + 1) * LANES] = rows[
                    at : at + own_rows
                ]

    def drain_orb(o):
        copy_a(o, me).wait_send()
        copy_i(o, me).wait_send()
        copy_d(o, me).wait_send()

    def drain_pair(q):
        copy_p(q, mine).wait_send()
        copy_t(q, mine).wait_send()

    each_orb(drain_orb)
    each_pair(drain_pair)


def local(n_orb, n_pair, orbitals, send_index, pair_left, pair_offset):
    owned, box_side, plane = orbitals.shape
    slots = send_index.shape[2]
    groups = plane // n_pair // LANES
    pad = box_side // 4
    own_rows = box_side // n_pair
    assert owned * 2 * box_side == LANES and slots == n_orb
    vmem = pl.BlockSpec(memory_space=pltpu.VMEM)
    bf16, f32, i32 = jnp.bfloat16, jnp.float32, jnp.int32
    dma = pltpu.SemaphoreType.DMA
    dense = (owned, groups, box_side, LANES)
    field = pl.pallas_call(
        functools.partial(kernel, n_orb, n_pair),
        out_shape=jax.ShapeDtypeStruct((owned, own_rows, plane), f32),
        in_specs=[vmem] * 4,
        out_specs=vmem,
        scratch_shapes=[
            pltpu.VMEM((owned + 1, groups + 1, box_side, LANES), f32),
            pltpu.VMEM((owned + 1, groups + 1, box_side + 2 * pad, LANES), f32),
            pltpu.VMEM((groups, box_side + 2 * SUBS, LANES), f32),
            pltpu.VMEM((groups, box_side + 2 * pad, LANES), f32),
            pltpu.VMEM(dense, f32),
            pltpu.VMEM(dense, f32),
            pltpu.VMEM((n_orb, owned * groups + 1, box_side, LANES), bf16),
            pltpu.VMEM((n_orb, *dense), bf16),
            pltpu.VMEM((n_orb, *dense), bf16),
            pltpu.VMEM((n_pair, owned * groups * own_rows, LANES), bf16),
            pltpu.VMEM((n_pair, owned * groups * own_rows, LANES), bf16),
            pltpu.VMEM((3, n_pair, 1, slots), i32),
            pltpu.VMEM((n_orb, n_pair, 1, slots), i32),
            pltpu.SMEM((3, n_pair, 1, slots), i32),
            pltpu.SMEM((n_orb, n_pair, 1, slots), i32),
            dma((n_orb,)),
            dma((n_orb,)),
            dma((n_orb,)),
            dma((n_orb,)),
            dma((n_pair,)),
            dma((n_pair,)),
            dma((n_pair,)),
            dma((n_pair,)),
            dma((n_orb,)),
            dma((n_orb,)),
            dma(()),
        ],
        compiler_params=pltpu.CompilerParams(collective_id=0, has_side_effects=True),
        name="exchange",
    )(orbitals, send_index, pair_left, pair_offset)
    return -0.25 * field


def solution(mesh):
    n_orb, n_pair = mesh.shape["orb"], mesh.shape["pair"]
    return jax.shard_map(
        functools.partial(local, n_orb, n_pair),
        mesh=mesh,
        in_specs=(
            P("orb", None, None),
            P("orb", "pair", None),
            P("orb", "pair", None),
            P("orb", "pair", None),
        ),
        out_specs=P("orb", "pair", None),
        check_vma=False,
    )
```

```python
import functools

import jax
import jax.numpy as jnp
from jax import lax
from jax.experimental import pallas as pl
from jax.experimental.pallas import tpu as pltpu
from jax.sharding import PartitionSpec as P

LANES = 128
SUBS = 8
SEND, LEFT, OFFSET = 0, 1, 2


def kernel(
    n_orb,
    n_pair,
    orb_ref,
    send_ref,
    left_ref,
    off_ref,
    out_ref,
    left_boxes,
    right_boxes,
    dens,
    prod,
    left_sum,
    right_sum,
    in_a,
    out_d,
    in_d,
    total,
    tab_pair,
    tab_orb,
    idx_pair,
    idx_orb,
    send_a,
    recv_a,
    send_d,
    recv_d,
    send_p,
    recv_p,
    send_i,
    recv_i,
    local_sem,
):
    owned, box_side, plane = orb_ref.shape
    groups = plane // n_pair // LANES
    pad = box_side // 4
    own_rows = box_side // n_pair
    f32, bf16 = jnp.float32, jnp.bfloat16
    me = lax.axis_index("orb")
    mine = lax.axis_index("pair")
    barrier = pltpu.get_barrier_semaphore()

    def each_orb(body):
        lax.fori_loop(1, n_orb, lambda k, c: (body(lax.rem(me + k, n_orb)), c)[1], 0)

    def each_pair(body):
        lax.fori_loop(1, n_pair, lambda k, c: (body(lax.rem(mine + k, n_pair)), c)[1], 0)

    def greet(k, c):
        other = lax.rem(me * n_pair + mine + k, n_orb * n_pair)
        pl.semaphore_signal(
            barrier, inc=1, device_id={"orb": other // n_pair, "pair": lax.rem(other, n_pair)}
        )
        return c

    lax.fori_loop(1, n_orb * n_pair, greet, 0)

    tab_pair[SEND, mine] = send_ref[0]
    tab_pair[LEFT, mine] = left_ref[0]
    tab_pair[OFFSET, mine] = off_ref[0]

    lane = lax.broadcasted_iota(jnp.int32, (box_side, LANES), 1)
    first = mine * groups
    below = jnp.maximum(first - 1, 0)
    above = jnp.minimum(first + groups, groups * n_pair - 1)

    def column(b, c):
        at = pl.ds(pl.multiple_of(c * LANES, LANES), LANES)
        return orb_ref[b, :, at].astype(bf16).astype(f32)

    left_boxes[0] = jnp.zeros(left_boxes.shape[1:], f32)
    right_boxes[...] = jnp.zeros(right_boxes.shape, f32)
    halos = []
    for b in range(owned):
        for g in range(groups):
            piece = column(b, first + g)
            left_boxes[b + 1, g] = piece
            in_a[me, b * groups + g] = piece.astype(bf16)
        has_below = lane + jnp.where(mine > 0, 0, LANES) < box_side
        has_above = lane - jnp.where(mine < n_pair - 1, 0, LANES) >= LANES - box_side
        halo = jnp.where(has_below, pltpu.roll(column(b, below), box_side, 1), 0.0)
        halo = jnp.where(
            has_above, pltpu.roll(column(b, above), LANES - box_side, 1), halo
        )
        left_boxes[b + 1, groups] = halo
        halos.append(halo if b == 0 else pltpu.roll(halo, b * 2 * box_side, 1))
    in_a[me, owned * groups] = functools.reduce(jnp.add, halos).astype(bf16)
    dens[...] = jnp.zeros(dens.shape, f32)
    prod[...] = jnp.zeros(prod.shape, f32)
    left_sum[...] = jnp.zeros(left_sum.shape, f32)

    pl.semaphore_wait(barrier, n_orb * n_pair - 1)

    def copy_p(q, row):
        return pltpu.make_async_remote_copy(
            src_ref=tab_pair.at[:, mine],
            dst_ref=tab_pair.at[:, row],
            send_sem=send_p.at[q],
            recv_sem=recv_p.at[row],
            device_id={"pair": q},
        )

    fold = 2 if n_orb % 2 == 0 else 1
    lines = n_orb // fold
    high, low = me // fold, lax.rem(me, fold)

    def copy_a(block, key, o):
        return pltpu.make_async_remote_copy(
            src_ref=in_a.at[block],
            dst_ref=in_a.at[block],
            send_sem=send_a.at[key],
            recv_sem=recv_a.at[block],
            device_id={"orb": o},
        )

    def peer(k, side):
        return lax.rem(high + k + lines, lines) * fold + lax.rem(low + side, fold)

    def along(body, start=1):
        lax.fori_loop(start, lines, lambda k, c: (body(k), c)[1], 0)

    def copy_i(o, slot):
        return pltpu.make_async_remote_copy(
            src_ref=tab_pair.at[SEND],
            dst_ref=tab_orb.at[slot],
            send_sem=send_i.at[o],
            recv_sem=recv_i.at[slot],
            device_id={"orb": o},
        )

    def copy_d(o, q, slot, row):
        return pltpu.make_async_remote_copy(
            src_ref=out_d.at[o, q],
            dst_ref=in_d.at[slot, row],
            send_sem=send_d.at[o, q],
            recv_sem=recv_d.at[slot, row],
            device_id={"orb": o, "pair": q},
        )

    each_pair(lambda q: copy_p(q, mine).start())
    if fold > 1:
        copy_a(me, peer(0, 1), peer(0, 1)).start()
    along(lambda k: copy_a(me, peer(k, 0), peer(k, 0)).start())
    each_pair(lambda q: copy_p(q, q).wait_recv())
    each_orb(lambda o: copy_i(o, me).start())
    tab_orb[me] = tab_pair[SEND]
    fetch = pltpu.make_async_copy(tab_pair, idx_pair, local_sem)
    fetch.start()
    fetch.wait()

    tile = (SUBS, LANES)
    lane = lax.broadcasted_iota(jnp.int32, tile, 1)
    inner_up = lane % box_side > 0
    inner_down = lane % box_side < box_side - 1
    from_here_up = lane >= box_side
    from_here_down = lane < LANES - box_side
    sixth = 1.0 / 6.0
    steps = box_side // SUBS

    def process(s, right_index):
        for b in range(owned):
            for g in range(groups):
                right_boxes[b + 1, g, pl.ds(pad, box_side), :] = in_a[s, b * groups + g].astype(f32)
            halo = in_a[s, owned * groups].astype(f32)
            if b:
                halo = pltpu.roll(halo, LANES - b * 2 * box_side, 1)
            right_boxes[b + 1, groups, pl.ds(pad, box_side), :] = halo
        right_sum[...] = jnp.zeros(right_sum.shape, f32)

        def route(p, c):
            right_pick = right_index(p)
            left_pick = idx_pair[LEFT, p, 0, s]
            t = idx_pair[OFFSET, p, 0, s]
            left_tile = jnp.full(tile, left_pick, jnp.int32)
            right_tile = jnp.full(tile, right_pick, jnp.int32)
            rights, lefts, q = {}, {}, {}
            for i in range(steps):
                for g in range(groups + 1):
                    right = right_boxes[right_pick + 1, g, pl.ds(pad + i * SUBS - t, SUBS), :]
                    left = left_boxes[left_pick + 1, g, pl.ds(i * SUBS, SUBS), :]
                    q[i, g] = left * right
                    if g < groups:
                        dens[g, pl.ds((i + 1) * SUBS, SUBS), :] = q[i, g]
                        rights[i, g], lefts[i, g] = right, left
            for i in range(steps):
                ups = [pltpu.roll(q[i, g], box_side, 1) for g in range(groups)]
                downs = [pltpu.roll(q[i, g], LANES - box_side, 1) for g in range(groups)]
                for g in range(groups):
                    here = q[i, g]
                    up = jnp.where(from_here_up, ups[g], ups[g - 1] if g else q[i, groups])
                    down = jnp.where(
                        from_here_down,
                        downs[g],
                        downs[g + 1] if g + 1 < groups else q[i, groups],
                    )
                    fore = jnp.where(inner_up, pltpu.roll(here, 1, 1), 0.0)
                    back = jnp.where(inner_down, pltpu.roll(here, LANES - 1, 1), 0.0)
                    before = dens[g, pl.ds((i + 1) * SUBS - 1, SUBS), :]
                    after = dens[g, pl.ds((i + 1) * SUBS + 1, SUBS), :]
                    around = (up + down) + (fore + back) + (before + after)
                    potential = (around * sixth + here) * sixth
                    to_left = potential * rights[i, g]
                    at = pl.ds(i * SUBS, SUBS)
                    for b in range(owned):
                        left_sum[b, g, at, :] = left_sum[b, g, at, :] + jnp.where(
                            left_tile == b, to_left, 0.0
                        )
                    prod[g, pl.ds(pad + i * SUBS, SUBS), :] = potential * lefts[i, g]
            for i in range(steps):
                at = pl.ds(i * SUBS, SUBS)
                for g in range(groups):
                    value = prod[g, pl.ds(pad + i * SUBS + t, SUBS), :]
                    for b in range(owned):
                        right_sum[b, g, at, :] = right_sum[b, g, at, :] + jnp.where(
                            right_tile == b, value, 0.0
                        )
            return c

        lax.fori_loop(0, n_pair, route, 0)

    process(me, lambda p: idx_pair[SEND, p, 0, me])
    left_sum[...] = left_sum[...] + right_sum[...]

    each_orb(lambda o: copy_i(o, o).wait_recv())
    fetch_orb = pltpu.make_async_copy(tab_orb, idx_orb, local_sem)
    fetch_orb.start()
    fetch_orb.wait()

    blocks = owned * groups

    def parts(ref, s):
        for q in range(n_pair):
            rows = ref[:, :, q * own_rows : (q + 1) * own_rows, :]
            out_d[s, q] = rows.reshape(blocks * own_rows, LANES).astype(bf16)

    def every(body):
        lax.fori_loop(0, n_pair, lambda q, c: (body(q), c)[1], 0)

    def slot(s):
        process(s, lambda p: idx_orb[s, p, 0, me])
        parts(right_sum, s)
        every(lambda q: copy_d(s, q, me, mine).start())

    def on_line(k):
        s = peer(-k, 0)
        copy_a(s, s, s).wait_recv()
        if fold > 1:
            copy_a(s, peer(-k, 1), peer(0, 1)).start()
        slot(s)

    def across(k):
        s = peer(-k, 1)
        copy_a(s, s, s).wait_recv()
        slot(s)

    along(on_line)
    if fold > 1:
        along(across, 0)

    parts(left_sum, me)
    each_pair(lambda q: copy_d(me, q, me, mine).start())
    for q in range(n_pair):
        total[q] = jnp.zeros(total.shape[1:], f32)
    total[mine] = out_d[me, mine].astype(f32)

    def add(s):
        def one(q):
            copy_d(s, q, s, q).wait_recv()
            total[q] = total[q] + in_d[s, q].astype(f32)

        return one

    each_orb(lambda s: every(add(s)))
    each_pair(add(me))
    for q in range(n_pair):
        for b in range(owned):
            for g in range(groups):
                at = (b * groups + g) * own_rows
                out_ref[b, :, (q * groups + g) * LANES : (q * groups + g + 1) * LANES] = total[
                    q, at : at + own_rows, :
                ]

    def drain_orb(o):
        copy_a(me, o, o).wait_send()
        copy_i(o, me).wait_send()
        every(lambda q: copy_d(o, q, me, mine).wait_send())

    def drain_pair(q):
        copy_p(q, mine).wait_send()
        copy_d(me, q, me, mine).wait_send()

    each_orb(drain_orb)
    each_pair(drain_pair)


def local(n_orb, n_pair, orbitals, send_index, pair_left, pair_offset):
    owned, box_side, plane = orbitals.shape
    slots = send_index.shape[2]
    groups = plane // n_pair // LANES
    pad = box_side // 4
    own_rows = box_side // n_pair
    assert owned * 2 * box_side == LANES and slots == n_orb
    vmem = pl.BlockSpec(memory_space=pltpu.VMEM)
    bf16, f32, i32 = jnp.bfloat16, jnp.float32, jnp.int32
    dma = pltpu.SemaphoreType.DMA
    dense = (owned, groups, box_side, LANES)
    field = pl.pallas_call(
        functools.partial(kernel, n_orb, n_pair),
        out_shape=jax.ShapeDtypeStruct((owned, own_rows, plane), f32),
        in_specs=[vmem] * 4,
        out_specs=vmem,
        scratch_shapes=[
            pltpu.VMEM((owned + 1, groups + 1, box_side, LANES), f32),
            pltpu.VMEM((owned + 1, groups + 1, box_side + 2 * pad, LANES), f32),
            pltpu.VMEM((groups, box_side + 2 * SUBS, LANES), f32),
            pltpu.VMEM((groups, box_side + 2 * pad, LANES), f32),
            pltpu.VMEM(dense, f32),
            pltpu.VMEM(dense, f32),
            pltpu.VMEM((n_orb, owned * groups + 1, box_side, LANES), bf16),
            pltpu.VMEM((n_orb, n_pair, owned * groups * own_rows, LANES), bf16),
            pltpu.VMEM((n_orb, n_pair, owned * groups * own_rows, LANES), bf16),
            pltpu.VMEM((n_pair, owned * groups * own_rows, LANES), f32),
            pltpu.VMEM((3, n_pair, 1, slots), i32),
            pltpu.VMEM((n_orb, n_pair, 1, slots), i32),
            pltpu.SMEM((3, n_pair, 1, slots), i32),
            pltpu.SMEM((n_orb, n_pair, 1, slots), i32),
            dma((n_orb,)),
            dma((n_orb,)),
            dma((n_orb, n_pair)),
            dma((n_orb, n_pair)),
            dma((n_pair,)),
            dma((n_pair,)),
            dma((n_orb,)),
            dma((n_orb,)),
            dma(()),
        ],
        compiler_params=pltpu.CompilerParams(collective_id=0, has_side_effects=True),
        name="exchange",
    )(orbitals, send_index, pair_left, pair_offset)
    return -0.25 * field


def solution(mesh):
    n_orb, n_pair = mesh.shape["orb"], mesh.shape["pair"]
    return jax.shard_map(
        functools.partial(local, n_orb, n_pair),
        mesh=mesh,
        in_specs=(
            P("orb", None, None),
            P("orb", "pair", None),
            P("orb", "pair", None),
            P("orb", "pair", None),
        ),
        out_specs=P("orb", "pair", None),
        check_vma=False,
    )
```

```python
import functools

import jax
import jax.numpy as jnp
from jax import lax
from jax.experimental import pallas as pl
from jax.experimental.pallas import tpu as pltpu
from jax.sharding import PartitionSpec as P

LANES = 128
SUBS = 8
LEFT, OFFSET = 0, 1


def kernel(
    n_orb,
    n_pair,
    orb_ref,
    send_ref,
    left_ref,
    off_ref,
    out_ref,
    left_boxes,
    right_boxes,
    dens,
    prod,
    left_sum,
    right_sum,
    in_a,
    out_d,
    in_d,
    total,
    tab_pair,
    tab_orb,
    idx_pair,
    idx_orb,
    send_a,
    recv_a,
    send_d,
    recv_d,
    send_p,
    recv_p,
    send_i,
    recv_i,
    local_sem,
):
    owned, box_side, plane = orb_ref.shape
    groups = plane // n_pair // LANES
    pad = box_side // 4
    own_rows = box_side // n_pair
    f32, bf16 = jnp.float32, jnp.bfloat16
    me = lax.axis_index("orb")
    mine = lax.axis_index("pair")
    barrier = pltpu.get_barrier_semaphore()

    def each_orb(body):
        lax.fori_loop(1, n_orb, lambda k, c: (body(lax.rem(me + k, n_orb)), c)[1], 0)

    def each_pair(body):
        lax.fori_loop(1, n_pair, lambda k, c: (body(lax.rem(mine + k, n_pair)), c)[1], 0)

    def greet(k, c):
        other = lax.rem(me * n_pair + mine + k, n_orb * n_pair)
        pl.semaphore_signal(
            barrier, inc=1, device_id={"orb": other // n_pair, "pair": lax.rem(other, n_pair)}
        )
        return c

    lax.fori_loop(1, n_orb * n_pair, greet, 0)

    tab_orb[me, mine] = send_ref[0]
    tab_pair[LEFT, mine] = left_ref[0]
    tab_pair[OFFSET, mine] = off_ref[0]

    lane = lax.broadcasted_iota(jnp.int32, (box_side, LANES), 1)
    first = mine * groups
    below = jnp.maximum(first - 1, 0)
    above = jnp.minimum(first + groups, groups * n_pair - 1)

    def column(b, c):
        at = pl.ds(pl.multiple_of(c * LANES, LANES), LANES)
        return orb_ref[b, :, at].astype(bf16).astype(f32)

    left_boxes[0] = jnp.zeros(left_boxes.shape[1:], f32)
    right_boxes[...] = jnp.zeros(right_boxes.shape, f32)
    halos = []
    for b in range(owned):
        for g in range(groups):
            piece = column(b, first + g)
            left_boxes[b + 1, g] = piece
            in_a[me, b * groups + g] = piece.astype(bf16)
        has_below = lane + jnp.where(mine > 0, 0, LANES) < box_side
        has_above = lane - jnp.where(mine < n_pair - 1, 0, LANES) >= LANES - box_side
        halo = jnp.where(has_below, pltpu.roll(column(b, below), box_side, 1), 0.0)
        halo = jnp.where(
            has_above, pltpu.roll(column(b, above), LANES - box_side, 1), halo
        )
        left_boxes[b + 1, groups] = halo
        halos.append(halo if b == 0 else pltpu.roll(halo, b * 2 * box_side, 1))
    in_a[me, owned * groups] = functools.reduce(jnp.add, halos).astype(bf16)
    dens[...] = jnp.zeros(dens.shape, f32)
    prod[...] = jnp.zeros(prod.shape, f32)
    left_sum[...] = jnp.zeros(left_sum.shape, f32)

    pl.semaphore_wait(barrier, n_orb * n_pair - 1)

    def copy_p(q, row):
        return pltpu.make_async_remote_copy(
            src_ref=tab_pair.at[:, mine],
            dst_ref=tab_pair.at[:, row],
            send_sem=send_p.at[q],
            recv_sem=recv_p.at[row],
            device_id={"pair": q},
        )

    fold = 2 if n_orb % 2 == 0 else 1
    lines = n_orb // fold
    high, low = me // fold, lax.rem(me, fold)

    def copy_a(block, key, o):
        return pltpu.make_async_remote_copy(
            src_ref=in_a.at[block],
            dst_ref=in_a.at[block],
            send_sem=send_a.at[key],
            recv_sem=recv_a.at[block],
            device_id={"orb": o},
        )

    def peer(k, side):
        return lax.rem(high + k + lines, lines) * fold + lax.rem(low + side, fold)

    def along(body, start=1):
        lax.fori_loop(start, lines, lambda k, c: (body(k), c)[1], 0)

    def copy_i(o, q, slot, row):
        return pltpu.make_async_remote_copy(
            src_ref=tab_orb.at[me, mine],
            dst_ref=tab_orb.at[slot, row],
            send_sem=send_i.at[o, q],
            recv_sem=recv_i.at[slot, row],
            device_id={"orb": o, "pair": q},
        )

    def every(body):
        lax.fori_loop(0, n_pair, lambda q, c: (body(q), c)[1], 0)

    def copy_d(o, q, slot, row):
        return pltpu.make_async_remote_copy(
            src_ref=out_d.at[o, q],
            dst_ref=in_d.at[slot, row],
            send_sem=send_d.at[o, q],
            recv_sem=recv_d.at[slot, row],
            device_id={"orb": o, "pair": q},
        )

    each_pair(lambda q: copy_p(q, mine).start())
    each_pair(lambda q: copy_i(me, q, me, mine).start())
    each_orb(lambda o: every(lambda q: copy_i(o, q, me, mine).start()))
    if fold > 1:
        copy_a(me, peer(0, 1), peer(0, 1)).start()
    along(lambda k: copy_a(me, peer(k, 0), peer(k, 0)).start())
    each_pair(lambda q: copy_p(q, q).wait_recv())
    each_pair(lambda q: copy_i(me, q, me, q).wait_recv())
    fetch = pltpu.make_async_copy(tab_pair, idx_pair, local_sem.at[0])
    fetch_own = pltpu.make_async_copy(tab_orb.at[me], idx_orb.at[me], local_sem.at[1])
    fetch.start()
    fetch_own.start()
    fetch.wait()
    fetch_own.wait()

    tile = (SUBS, LANES)
    lane = lax.broadcasted_iota(jnp.int32, tile, 1)
    inner_up = lane % box_side > 0
    inner_down = lane % box_side < box_side - 1
    from_here_up = lane >= box_side
    from_here_down = lane < LANES - box_side
    sixth = 1.0 / 6.0
    steps = box_side // SUBS

    def process(s, right_index):
        for b in range(owned):
            for g in range(groups):
                right_boxes[b + 1, g, pl.ds(pad, box_side), :] = in_a[s, b * groups + g].astype(f32)
            halo = in_a[s, owned * groups].astype(f32)
            if b:
                halo = pltpu.roll(halo, LANES - b * 2 * box_side, 1)
            right_boxes[b + 1, groups, pl.ds(pad, box_side), :] = halo
        right_sum[...] = jnp.zeros(right_sum.shape, f32)

        def route(p, c):
            right_pick = right_index(p)
            left_pick = idx_pair[LEFT, p, 0, s]
            t = idx_pair[OFFSET, p, 0, s]
            left_tile = jnp.full(tile, left_pick, jnp.int32)
            right_tile = jnp.full(tile, right_pick, jnp.int32)
            rights, lefts, q = {}, {}, {}
            for i in range(steps):
                for g in range(groups + 1):
                    right = right_boxes[right_pick + 1, g, pl.ds(pad + i * SUBS - t, SUBS), :]
                    left = left_boxes[left_pick + 1, g, pl.ds(i * SUBS, SUBS), :]
                    q[i, g] = left * right
                    if g < groups:
                        dens[g, pl.ds((i + 1) * SUBS, SUBS), :] = q[i, g]
                        rights[i, g], lefts[i, g] = right, left
            for i in range(steps):
                ups = [pltpu.roll(q[i, g], box_side, 1) for g in range(groups)]
                downs = [pltpu.roll(q[i, g], LANES - box_side, 1) for g in range(groups)]
                for g in range(groups):
                    here = q[i, g]
                    up = jnp.where(from_here_up, ups[g], ups[g - 1] if g else q[i, groups])
                    down = jnp.where(
                        from_here_down,
                        downs[g],
                        downs[g + 1] if g + 1 < groups else q[i, groups],
                    )
                    fore = jnp.where(inner_up, pltpu.roll(here, 1, 1), 0.0)
                    back = jnp.where(inner_down, pltpu.roll(here, LANES - 1, 1), 0.0)
                    before = dens[g, pl.ds((i + 1) * SUBS - 1, SUBS), :]
                    after = dens[g, pl.ds((i + 1) * SUBS + 1, SUBS), :]
                    around = (up + down) + (fore + back) + (before + after)
                    potential = (around * sixth + here) * sixth
                    to_left = potential * rights[i, g]
                    at = pl.ds(i * SUBS, SUBS)
                    for b in range(owned):
                        left_sum[b, g, at, :] = left_sum[b, g, at, :] + jnp.where(
                            left_tile == b, to_left, 0.0
                        )
                    prod[g, pl.ds(pad + i * SUBS, SUBS), :] = potential * lefts[i, g]
            for i in range(steps):
                at = pl.ds(i * SUBS, SUBS)
                for g in range(groups):
                    value = prod[g, pl.ds(pad + i * SUBS + t, SUBS), :]
                    for b in range(owned):
                        right_sum[b, g, at, :] = right_sum[b, g, at, :] + jnp.where(
                            right_tile == b, value, 0.0
                        )
            return c

        lax.fori_loop(0, n_pair, route, 0)

    process(me, lambda p: idx_orb[me, p, 0, me])
    left_sum[...] = left_sum[...] + right_sum[...]

    each_orb(lambda o: every(lambda q: copy_i(o, q, o, q).wait_recv()))
    fetch_orb = pltpu.make_async_copy(tab_orb, idx_orb, local_sem.at[0])
    fetch_orb.start()
    fetch_orb.wait()

    blocks = owned * groups

    def parts(ref, s):
        for q in range(n_pair):
            rows = ref[:, :, q * own_rows : (q + 1) * own_rows, :]
            out_d[s, q] = rows.reshape(blocks * own_rows, LANES).astype(bf16)

    def slot(s):
        process(s, lambda p: idx_orb[s, p, 0, me])
        parts(right_sum, s)
        every(lambda q: copy_d(s, q, me, mine).start())

    def on_line(k):
        s = peer(-k, 0)
        copy_a(s, s, s).wait_recv()
        if fold > 1:
            copy_a(s, peer(-k, 1), peer(0, 1)).start()
        slot(s)

    def across(k):
        s = peer(-k, 1)
        copy_a(s, s, s).wait_recv()
        slot(s)

    along(on_line)
    if fold > 1:
        along(across, 0)

    parts(left_sum, me)
    each_pair(lambda q: copy_d(me, q, me, mine).start())
    for q in range(n_pair):
        total[q] = jnp.zeros(total.shape[1:], f32)
    total[mine] = out_d[me, mine].astype(f32)

    def add(s):
        def one(q):
            copy_d(s, q, s, q).wait_recv()
            total[q] = total[q] + in_d[s, q].astype(f32)

        return one

    each_orb(lambda s: every(add(s)))
    each_pair(add(me))
    for q in range(n_pair):
        for b in range(owned):
            for g in range(groups):
                at = (b * groups + g) * own_rows
                out_ref[b, :, (q * groups + g) * LANES : (q * groups + g + 1) * LANES] = total[
                    q, at : at + own_rows, :
                ]

    def drain_orb(o):
        copy_a(me, o, o).wait_send()
        every(lambda q: copy_i(o, q, me, mine).wait_send())
        every(lambda q: copy_d(o, q, me, mine).wait_send())

    def drain_pair(q):
        copy_p(q, mine).wait_send()
        copy_i(me, q, me, mine).wait_send()
        copy_d(me, q, me, mine).wait_send()

    each_orb(drain_orb)
    each_pair(drain_pair)


def local(n_orb, n_pair, orbitals, send_index, pair_left, pair_offset):
    owned, box_side, plane = orbitals.shape
    slots = send_index.shape[2]
    groups = plane // n_pair // LANES
    pad = box_side // 4
    own_rows = box_side // n_pair
    assert owned * 2 * box_side == LANES and slots == n_orb
    vmem = pl.BlockSpec(memory_space=pltpu.VMEM)
    bf16, f32, i32 = jnp.bfloat16, jnp.float32, jnp.int32
    dma = pltpu.SemaphoreType.DMA
    dense = (owned, groups, box_side, LANES)
    field = pl.pallas_call(
        functools.partial(kernel, n_orb, n_pair),
        out_shape=jax.ShapeDtypeStruct((owned, own_rows, plane), f32),
        in_specs=[vmem] * 4,
        out_specs=vmem,
        scratch_shapes=[
            pltpu.VMEM((owned + 1, groups + 1, box_side, LANES), f32),
            pltpu.VMEM((owned + 1, groups + 1, box_side + 2 * pad, LANES), f32),
            pltpu.VMEM((groups, box_side + 2 * SUBS, LANES), f32),
            pltpu.VMEM((groups, box_side + 2 * pad, LANES), f32),
            pltpu.VMEM(dense, f32),
            pltpu.VMEM(dense, f32),
            pltpu.VMEM((n_orb, owned * groups + 1, box_side, LANES), bf16),
            pltpu.VMEM((n_orb, n_pair, owned * groups * own_rows, LANES), bf16),
            pltpu.VMEM((n_orb, n_pair, owned * groups * own_rows, LANES), bf16),
            pltpu.VMEM((n_pair, owned * groups * own_rows, LANES), f32),
            pltpu.VMEM((2, n_pair, 1, slots), i32),
            pltpu.VMEM((n_orb, n_pair, 1, slots), i32),
            pltpu.SMEM((2, n_pair, 1, slots), i32),
            pltpu.SMEM((n_orb, n_pair, 1, slots), i32),
            dma((n_orb,)),
            dma((n_orb,)),
            dma((n_orb, n_pair)),
            dma((n_orb, n_pair)),
            dma((n_pair,)),
            dma((n_pair,)),
            dma((n_orb, n_pair)),
            dma((n_orb, n_pair)),
            dma((2,)),
        ],
        compiler_params=pltpu.CompilerParams(collective_id=0, has_side_effects=True),
        name="exchange",
    )(orbitals, send_index, pair_left, pair_offset)
    return -0.25 * field


def solution(mesh):
    n_orb, n_pair = mesh.shape["orb"], mesh.shape["pair"]
    return jax.shard_map(
        functools.partial(local, n_orb, n_pair),
        mesh=mesh,
        in_specs=(
            P("orb", None, None),
            P("orb", "pair", None),
            P("orb", "pair", None),
            P("orb", "pair", None),
        ),
        out_specs=P("orb", "pair", None),
        check_vma=False,
    )
```

```python
import functools

import jax
import jax.numpy as jnp
from jax import lax
from jax.experimental import pallas as pl
from jax.experimental.pallas import tpu as pltpu
from jax.sharding import PartitionSpec as P

LANES = 128
SUBS = 8
LEFT, OFFSET = 0, 1


def kernel(
    n_orb,
    n_pair,
    orb_ref,
    send_ref,
    left_ref,
    off_ref,
    out_ref,
    left_boxes,
    right_boxes,
    dens,
    prod,
    left_sum,
    right_sum,
    in_a,
    out_d,
    in_d,
    total,
    tab_pair,
    tab_orb,
    idx_pair,
    idx_orb,
    send_a,
    recv_a,
    send_d,
    recv_d,
    send_p,
    recv_p,
    send_i,
    recv_i,
    local_sem,
):
    owned, box_side, plane = orb_ref.shape
    groups = plane // n_pair // LANES
    pad = box_side // 4
    own_rows = box_side // n_pair
    f32, bf16 = jnp.float32, jnp.bfloat16
    me = lax.axis_index("orb")
    mine = lax.axis_index("pair")
    barrier = pltpu.get_barrier_semaphore()

    def each_orb(body):
        lax.fori_loop(1, n_orb, lambda k, c: (body(lax.rem(me + k, n_orb)), c)[1], 0)

    def each_pair(body):
        lax.fori_loop(1, n_pair, lambda k, c: (body(lax.rem(mine + k, n_pair)), c)[1], 0)

    def greet(k, c):
        other = lax.rem(me * n_pair + mine + k, n_orb * n_pair)
        pl.semaphore_signal(
            barrier, inc=1, device_id={"orb": other // n_pair, "pair": lax.rem(other, n_pair)}
        )
        return c

    lax.fori_loop(1, n_orb * n_pair, greet, 0)

    tab_orb[me, mine] = send_ref[0]
    tab_pair[LEFT, mine] = left_ref[0]
    tab_pair[OFFSET, mine] = off_ref[0]

    lane = lax.broadcasted_iota(jnp.int32, (box_side, LANES), 1)
    first = mine * groups
    below = jnp.maximum(first - 1, 0)
    above = jnp.minimum(first + groups, groups * n_pair - 1)

    def column(b, c):
        at = pl.ds(pl.multiple_of(c * LANES, LANES), LANES)
        return orb_ref[b, :, at].astype(bf16).astype(f32)

    left_boxes[0] = jnp.zeros(left_boxes.shape[1:], f32)
    right_boxes[...] = jnp.zeros(right_boxes.shape, f32)
    halos = []
    for b in range(owned):
        for g in range(groups):
            piece = column(b, first + g)
            left_boxes[b + 1, g] = piece
            in_a[me, b * groups + g] = piece.astype(bf16)
        has_below = lane + jnp.where(mine > 0, 0, LANES) < box_side
        has_above = lane - jnp.where(mine < n_pair - 1, 0, LANES) >= LANES - box_side
        halo = jnp.where(has_below, pltpu.roll(column(b, below), box_side, 1), 0.0)
        halo = jnp.where(
            has_above, pltpu.roll(column(b, above), LANES - box_side, 1), halo
        )
        left_boxes[b + 1, groups] = halo
        halos.append(halo if b == 0 else pltpu.roll(halo, b * 2 * box_side, 1))
    in_a[me, owned * groups] = functools.reduce(jnp.add, halos).astype(bf16)
    dens[...] = jnp.zeros(dens.shape, f32)
    prod[...] = jnp.zeros(prod.shape, f32)
    left_sum[...] = jnp.zeros(left_sum.shape, f32)

    pl.semaphore_wait(barrier, n_orb * n_pair - 1)

    def copy_p(q, row):
        return pltpu.make_async_remote_copy(
            src_ref=tab_pair.at[:, mine],
            dst_ref=tab_pair.at[:, row],
            send_sem=send_p.at[q],
            recv_sem=recv_p.at[row],
            device_id={"pair": q},
        )

    fold = 2 if n_orb % 2 == 0 else 1
    lines = n_orb // fold
    high, low = me // fold, lax.rem(me, fold)

    def copy_a(block, key, o):
        return pltpu.make_async_remote_copy(
            src_ref=in_a.at[block],
            dst_ref=in_a.at[block],
            send_sem=send_a.at[key],
            recv_sem=recv_a.at[block],
            device_id={"orb": o},
        )

    def peer(k, side):
        return lax.rem(high + k + lines, lines) * fold + lax.rem(low + side, fold)

    def along(body, start=1):
        lax.fori_loop(start, lines, lambda k, c: (body(k), c)[1], 0)

    def copy_i(o, q, slot, row):
        return pltpu.make_async_remote_copy(
            src_ref=tab_orb.at[me, mine],
            dst_ref=tab_orb.at[slot, row],
            send_sem=send_i.at[o, q],
            recv_sem=recv_i.at[slot, row],
            device_id={"orb": o, "pair": q},
        )

    def every(body):
        lax.fori_loop(0, n_pair, lambda q, c: (body(q), c)[1], 0)

    def copy_d(o, q, slot, row):
        return pltpu.make_async_remote_copy(
            src_ref=out_d.at[o, q],
            dst_ref=in_d.at[slot, row],
            send_sem=send_d.at[o, q],
            recv_sem=recv_d.at[slot, row],
            device_id={"orb": o, "pair": q},
        )

    each_pair(lambda q: copy_p(q, mine).start())
    each_pair(lambda q: copy_i(me, q, me, mine).start())
    each_orb(lambda o: every(lambda q: copy_i(o, q, me, mine).start()))
    if fold > 1:
        copy_a(me, peer(0, 1), peer(0, 1)).start()
    along(lambda k: copy_a(me, peer(k, 0), peer(k, 0)).start())
    def hand_over(k):
        s = peer(-k, 0)
        copy_a(s, s, s).wait_recv()
        if fold > 1:
            copy_a(s, peer(-k, 1), peer(0, 1)).start()

    if lines > 1:
        hand_over(1)
    each_pair(lambda q: copy_p(q, q).wait_recv())
    each_pair(lambda q: copy_i(me, q, me, q).wait_recv())
    fetch = pltpu.make_async_copy(tab_pair, idx_pair, local_sem.at[0])
    fetch_own = pltpu.make_async_copy(tab_orb.at[me], idx_orb.at[me], local_sem.at[1])
    fetch.start()
    fetch_own.start()
    fetch.wait()
    fetch_own.wait()

    tile = (SUBS, LANES)
    lane = lax.broadcasted_iota(jnp.int32, tile, 1)
    inner_up = lane % box_side > 0
    inner_down = lane % box_side < box_side - 1
    from_here_up = lane >= box_side
    from_here_down = lane < LANES - box_side
    sixth = 1.0 / 6.0
    steps = box_side // SUBS

    def process(s, right_index):
        for b in range(owned):
            for g in range(groups):
                right_boxes[b + 1, g, pl.ds(pad, box_side), :] = in_a[s, b * groups + g].astype(f32)
            halo = in_a[s, owned * groups].astype(f32)
            if b:
                halo = pltpu.roll(halo, LANES - b * 2 * box_side, 1)
            right_boxes[b + 1, groups, pl.ds(pad, box_side), :] = halo
        right_sum[...] = jnp.zeros(right_sum.shape, f32)

        def route(p, c):
            right_pick = right_index(p)
            left_pick = idx_pair[LEFT, p, 0, s]
            t = idx_pair[OFFSET, p, 0, s]
            left_tile = jnp.full(tile, left_pick, jnp.int32)
            right_tile = jnp.full(tile, right_pick, jnp.int32)
            rights, lefts, q = {}, {}, {}
            for i in range(steps):
                for g in range(groups + 1):
                    right = right_boxes[right_pick + 1, g, pl.ds(pad + i * SUBS - t, SUBS), :]
                    left = left_boxes[left_pick + 1, g, pl.ds(i * SUBS, SUBS), :]
                    q[i, g] = left * right
                    if g < groups:
                        dens[g, pl.ds((i + 1) * SUBS, SUBS), :] = q[i, g]
                        rights[i, g], lefts[i, g] = right, left
            for i in range(steps):
                ups = [pltpu.roll(q[i, g], box_side, 1) for g in range(groups)]
                downs = [pltpu.roll(q[i, g], LANES - box_side, 1) for g in range(groups)]
                for g in range(groups):
                    here = q[i, g]
                    up = jnp.where(from_here_up, ups[g], ups[g - 1] if g else q[i, groups])
                    down = jnp.where(
                        from_here_down,
                        downs[g],
                        downs[g + 1] if g + 1 < groups else q[i, groups],
                    )
                    fore = jnp.where(inner_up, pltpu.roll(here, 1, 1), 0.0)
                    back = jnp.where(inner_down, pltpu.roll(here, LANES - 1, 1), 0.0)
                    before = dens[g, pl.ds((i + 1) * SUBS - 1, SUBS), :]
                    after = dens[g, pl.ds((i + 1) * SUBS + 1, SUBS), :]
                    around = (up + down) + (fore + back) + (before + after)
                    potential = (around * sixth + here) * sixth
                    to_left = potential * rights[i, g]
                    at = pl.ds(i * SUBS, SUBS)
                    for b in range(owned):
                        left_sum[b, g, at, :] = left_sum[b, g, at, :] + jnp.where(
                            left_tile == b, to_left, 0.0
                        )
                    prod[g, pl.ds(pad + i * SUBS, SUBS), :] = potential * lefts[i, g]
            for i in range(steps):
                at = pl.ds(i * SUBS, SUBS)
                for g in range(groups):
                    value = prod[g, pl.ds(pad + i * SUBS + t, SUBS), :]
                    for b in range(owned):
                        right_sum[b, g, at, :] = right_sum[b, g, at, :] + jnp.where(
                            right_tile == b, value, 0.0
                        )
            return c

        lax.fori_loop(0, n_pair, route, 0)

    process(me, lambda p: idx_orb[me, p, 0, me])
    left_sum[...] = left_sum[...] + right_sum[...]

    each_orb(lambda o: every(lambda q: copy_i(o, q, o, q).wait_recv()))
    fetch_orb = pltpu.make_async_copy(tab_orb, idx_orb, local_sem.at[0])
    fetch_orb.start()
    fetch_orb.wait()

    blocks = owned * groups

    def parts(ref, s):
        for q in range(n_pair):
            rows = ref[:, :, q * own_rows : (q + 1) * own_rows, :]
            out_d[s, q] = rows.reshape(blocks * own_rows, LANES).astype(bf16)

    def slot(s):
        process(s, lambda p: idx_orb[s, p, 0, me])
        parts(right_sum, s)
        every(lambda q: copy_d(s, q, me, mine).start())

    def on_line(k):
        @pl.when(k + 1 < lines)
        def _():
            hand_over(k + 1)

        slot(peer(-k, 0))

    def across(k):
        s = peer(-k, 1)
        copy_a(s, s, s).wait_recv()
        slot(s)

    along(on_line)
    if fold > 1:
        along(across, 0)

    parts(left_sum, me)
    each_pair(lambda q: copy_d(me, q, me, mine).start())
    for q in range(n_pair):
        total[q] = jnp.zeros(total.shape[1:], f32)
    total[mine] = out_d[me, mine].astype(f32)

    def add(s):
        def one(q):
            copy_d(s, q, s, q).wait_recv()
            total[q] = total[q] + in_d[s, q].astype(f32)

        return one

    each_orb(lambda s: every(add(s)))
    each_pair(add(me))
    for q in range(n_pair):
        for b in range(owned):
            for g in range(groups):
                at = (b * groups + g) * own_rows
                out_ref[b, :, (q * groups + g) * LANES : (q * groups + g + 1) * LANES] = total[
                    q, at : at + own_rows, :
                ]

    def drain_orb(o):
        copy_a(me, o, o).wait_send()
        every(lambda q: copy_i(o, q, me, mine).wait_send())
        every(lambda q: copy_d(o, q, me, mine).wait_send())

    def drain_pair(q):
        copy_p(q, mine).wait_send()
        copy_i(me, q, me, mine).wait_send()
        copy_d(me, q, me, mine).wait_send()

    each_orb(drain_orb)
    each_pair(drain_pair)


def local(n_orb, n_pair, orbitals, send_index, pair_left, pair_offset):
    owned, box_side, plane = orbitals.shape
    slots = send_index.shape[2]
    groups = plane // n_pair // LANES
    pad = box_side // 4
    own_rows = box_side // n_pair
    assert owned * 2 * box_side == LANES and slots == n_orb
    vmem = pl.BlockSpec(memory_space=pltpu.VMEM)
    bf16, f32, i32 = jnp.bfloat16, jnp.float32, jnp.int32
    dma = pltpu.SemaphoreType.DMA
    dense = (owned, groups, box_side, LANES)
    field = pl.pallas_call(
        functools.partial(kernel, n_orb, n_pair),
        out_shape=jax.ShapeDtypeStruct((owned, own_rows, plane), f32),
        in_specs=[vmem] * 4,
        out_specs=vmem,
        scratch_shapes=[
            pltpu.VMEM((owned + 1, groups + 1, box_side, LANES), f32),
            pltpu.VMEM((owned + 1, groups + 1, box_side + 2 * pad, LANES), f32),
            pltpu.VMEM((groups, box_side + 2 * SUBS, LANES), f32),
            pltpu.VMEM((groups, box_side + 2 * pad, LANES), f32),
            pltpu.VMEM(dense, f32),
            pltpu.VMEM(dense, f32),
            pltpu.VMEM((n_orb, owned * groups + 1, box_side, LANES), bf16),
            pltpu.VMEM((n_orb, n_pair, owned * groups * own_rows, LANES), bf16),
            pltpu.VMEM((n_orb, n_pair, owned * groups * own_rows, LANES), bf16),
            pltpu.VMEM((n_pair, owned * groups * own_rows, LANES), f32),
            pltpu.VMEM((2, n_pair, 1, slots), i32),
            pltpu.VMEM((n_orb, n_pair, 1, slots), i32),
            pltpu.SMEM((2, n_pair, 1, slots), i32),
            pltpu.SMEM((n_orb, n_pair, 1, slots), i32),
            dma((n_orb,)),
            dma((n_orb,)),
            dma((n_orb, n_pair)),
            dma((n_orb, n_pair)),
            dma((n_pair,)),
            dma((n_pair,)),
            dma((n_orb, n_pair)),
            dma((n_orb, n_pair)),
            dma((2,)),
        ],
        compiler_params=pltpu.CompilerParams(collective_id=0, has_side_effects=True),
        name="exchange",
    )(orbitals, send_index, pair_left, pair_offset)
    return -0.25 * field


def solution(mesh):
    n_orb, n_pair = mesh.shape["orb"], mesh.shape["pair"]
    return jax.shard_map(
        functools.partial(local, n_orb, n_pair),
        mesh=mesh,
        in_specs=(
            P("orb", None, None),
            P("orb", "pair", None),
            P("orb", "pair", None),
            P("orb", "pair", None),
        ),
        out_specs=P("orb", "pair", None),
        check_vma=False,
    )
```
